32 devices in a mesh: group: 2 (over y), member: 4 (over z), strip: 2 (over x), sub: 2 (over core).
Axes of the slice: x: 2, y: 2, z: 4, core: 2. Of those that a mesh axis runs over, the one named last changes fastest.
Arguments:
- noisy: bfloat16 [8, 128, 128, 256], P(('group', 'member'), None, 'strip', 'sub'), parts along dimension 0, may hold values from -6 to 6
- condition: bfloat16 [24, 128, 256], P('group', ('strip', 'member'), 'sub'), parts along dimension 0, may hold values from -6 to 6
- levels: int32 [8], P(('group', 'member')), parts along dimension 0, may hold values from 0 to 17
- enc_w1: bfloat16 [9, 128, 12], replicated, may hold values from -0.625 to 0.625
- enc_b1: float32 [128], replicated, may hold values from -4 to 4
- enc_w2: bfloat16 [9, 128, 128], replicated, may hold values from -0.1875 to 0.1875
- enc_b2: float32 [128], replicated, may hold values from -4 to 4
- den_wa: bfloat16 [9, 128, 256], replicated, may hold values from -0.125 to 0.125
- den_ba: float32 [128], replicated, may hold values from -4 to 4
- noise_gain: float32 [128], replicated, may hold values from -6 to 6
- den_wb: bfloat16 [9, 128, 128], replicated, may hold values from -0.1875 to 0.1875
Outputs:
- denoised: bfloat16 [8, 128, 128, 256], P(('group', 'member'), None, 'strip', 'sub'), parts along dimension 0
The draws below stay inside these ranges and needn't reach their ends.
There are 2 independent parts, one for each index of `group`. The reference program is written for one: setup_inputs(seed, part) draws one part's arguments, and reference() takes and returns one part's arrays. A program takes and returns all parts, laid end to end along the dimension named above; an argument that names none is the same for every part. Nothing has to cross between parts.
All inputs are finite; a program needn't handle non-finite values.
Results may differ from the reference program's by a relative error of at most 0.0043.
The reference program's roundings to bfloat16 on the way (of `enc_first`, `features`, `joined` and `hidden`) count: a program that leaves them out, or rounds other values in their place, can miss the bound.
Values may be sent and summed in bfloat16 or wider, within the bound.
A program may use at most 64 MiB of HBM per device.

```python
import jax
import jax.numpy as jnp
from jax import lax

C = 128
CIN = 12
LEVELS = 18
MEMBERS = 4
H = 128
W = 256


def set_ends(entries, key, low, largest):
    longest = entries.shape.index(max(entries.shape))
    spots = []
    for shift in (0, 1):
        where = [jax.random.randint(jax.random.fold_in(key, axis), (), 0, length) for axis, length in enumerate(entries.shape)]
        where[longest] = (where[longest] + shift) % entries.shape[longest]
        spots.append(tuple(where))
    return entries.at[spots[0]].set(low).at[spots[1]].set(largest)


def block_scale(rng, dims, split, smallest, largest):
    def one(axis_at, blocks):
        heights = jax.random.uniform(jax.random.fold_in(jax.random.fold_in(rng, 6), axis_at), (blocks,), jnp.float32, smallest / len(split), largest / len(split))
        return jnp.repeat(jnp.exp(heights), dims[axis_at] // blocks).reshape((-1,) + (1,) * (len(dims) - axis_at - 1))

    factor_of = one(*split[0])
    for cut in split[1:]:
        factor_of = factor_of * one(*cut)
    return factor_of


def scatter_about(own_key, dims, deviation, bound, pieces=(), held_as=jnp.bfloat16):
    drawn = deviation * jax.random.normal(own_key, dims, jnp.float32)
    if pieces:
        drawn = drawn * block_scale(own_key, dims, pieces, -0.22, 0.18)
    return jnp.clip(drawn, -bound, bound).astype(held_as)


def setup_inputs(seed: int = 0, part: int = 0) -> dict:
    key_list = jax.random.split(jax.random.key(seed), 12)
    part_splits = jax.random.split(jax.random.fold_in(key_list[11], part), 12)
    return {
        "noisy": scatter_about(part_splits[0], (MEMBERS, C, H, W), 1.0, 6.0, ((0, 4), (2, 2), (3, 2))),
        "condition": scatter_about(part_splits[1], (CIN, H, W), 1.0, 6.0, ((1, 8), (2, 2))),
        "levels": set_ends(jax.random.randint(part_splits[2], (MEMBERS,), 0, LEVELS), jax.random.fold_in(part_splits[2], 1), 0, LEVELS - 1).astype(jnp.int32),
        "enc_w1": scatter_about(key_list[3], (9, C, CIN), (9 * CIN) ** -0.5, 0.625),
        "enc_b1": scatter_about(key_list[4], (C,), 1.0, 4.0, (), jnp.float32),
        "enc_w2": scatter_about(key_list[5], (9, C, C), (9 * C) ** -0.5, 0.1875),
        "enc_b2": scatter_about(key_list[6], (C,), 1.0, 4.0, (), jnp.float32),
        "den_wa": scatter_about(key_list[7], (9, C, 2 * C), (18 * C) ** -0.5, 0.125),
        "den_ba": scatter_about(key_list[8], (C,), 1.0, 4.0, (), jnp.float32),
        "noise_gain": scatter_about(key_list[9], (C,), 1.5, 6.0, (), jnp.float32),
        "den_wb": scatter_about(key_list[10], (9, C, C), (9 * C) ** -0.5, 0.1875),
    }


SIGMA_DATA = 0.5
SIG_LOW = 0.25
SIG_HIGH = 4.0

def conv_taps(padded, weight, out_rows, out_cols):
    summed = jnp.zeros((weight.shape[1], out_rows, out_cols), jnp.float32)
    for tap_index in range(9):
        row_shift = tap_index // 3
        col_shift = tap_index % 3
        shifted = padded[:, row_shift:row_shift + out_rows, col_shift:col_shift + out_cols].astype(jnp.float32)
        summed = summed + jnp.einsum('oc,crw->orw', weight[tap_index].astype(jnp.float32), shifted)
    return summed

def pad_cells(field):
    return jnp.pad(field, ((0, 0), (1, 1), (1, 1)))

def reference(noisy, condition, levels, enc_w1, enc_b1, enc_w2, enc_b2, den_wa, den_ba, noise_gain, den_wb):
    enc_first = jax.nn.silu(conv_taps(pad_cells(condition), enc_w1, H, W) + enc_b1[:, None, None]).astype(jnp.bfloat16)
    enc_first = lax.optimization_barrier(enc_first)
    features = (conv_taps(pad_cells(enc_first), enc_w2, H, W) + enc_b2[:, None, None]).astype(jnp.bfloat16)
    features = lax.optimization_barrier(features)

    def one_member(packed):
        member_field, level_index = packed
        noise_sigma = SIG_LOW * (SIG_HIGH / SIG_LOW) ** (level_index.astype(jnp.float32) / (LEVELS - 1))
        spread = noise_sigma * noise_sigma + SIGMA_DATA * SIGMA_DATA
        c_in = 1.0 / jnp.sqrt(spread)
        c_skip = SIGMA_DATA * SIGMA_DATA / spread
        c_out = noise_sigma * SIGMA_DATA / jnp.sqrt(spread)
        c_noise = jnp.log(noise_sigma) / 4.0
        scaled = (c_in * member_field.astype(jnp.float32)).astype(jnp.bfloat16)
        joined = lax.optimization_barrier(jnp.concatenate([scaled, features], axis=0))
        before = conv_taps(pad_cells(joined), den_wa, H, W) + den_ba[:, None, None] + c_noise * noise_gain[:, None, None]
        hidden = lax.optimization_barrier(jax.nn.silu(before).astype(jnp.bfloat16))
        update = conv_taps(pad_cells(hidden), den_wb, H, W)
        return (c_skip * member_field.astype(jnp.float32) + c_out * update).astype(jnp.bfloat16)
    return lax.map(one_member, (noisy, levels))
```

```python
import functools

import jax
import jax.numpy as jnp
from jax import lax
from jax.experimental import pallas as pl
from jax.experimental.pallas import tpu as pltpu
from jax.sharding import PartitionSpec as P

LEVELS = 18
SIGMA_DATA = 0.5
SIG_LOW = 0.25
SIG_HIGH = 4.0
SIDE = 8
DEEP = 4
NEAR = 2
CH = 16
MESH = pl.DeviceIdType.MESH
DIRS = [(a, b) for a in (-1, 0, 1) for b in (-1, 0, 1) if (a, b) != (0, 0)]


def exchange_kernel(
    members, strips, subs, cond_ref, noisy_ref, cond_out, rows_out, cols_out,
    own_sem, gather_send, gather_recv, cond_send, cond_recv, noisy_send, noisy_recv,
):
    member = lax.axis_index("member")
    strip = lax.axis_index("strip")
    sub = lax.axis_index("sub")
    share, _, width = cond_ref.shape
    rows = share * members
    cols = noisy_ref.shape[1]

    def beside(a, b):
        return {
            "strip": lax.rem(strip + a + strips, strips),
            "sub": lax.rem(sub + b + subs, subs),
        }

    mine = cond_out.at[pl.ds(DEEP + member * share, share), :, pl.ds(width, width)]
    own = pltpu.make_async_copy(cond_ref, mine, own_sem)
    own.start()

    barrier = pltpu.get_barrier_semaphore()
    for step in range(1, members):
        pl.semaphore_signal(
            barrier, inc=1, device_id={"member": lax.rem(member + step, members)},
            device_id_type=MESH,
        )
    for a, b in DIRS:
        pl.semaphore_signal(barrier, inc=1, device_id=beside(a, b), device_id_type=MESH)
    pl.semaphore_wait(barrier, members - 1 + len(DIRS))

    gathers = []
    for step in range(1, members):
        copy = pltpu.make_async_remote_copy(
            src_ref=cond_ref, dst_ref=mine,
            send_sem=gather_send.at[step], recv_sem=gather_recv.at[step],
            device_id={"member": lax.rem(member + step, members)}, device_id_type=MESH,
        )
        copy.start()
        gathers.append(copy)

    fields = []
    for at, (a, b) in enumerate(DIRS):
        src_col = 0 if b < 0 else (cols - SIDE if b > 0 else 0)
        dst_col = SIDE + cols if b < 0 else (0 if b > 0 else SIDE)
        col_n = SIDE if b else cols
        if a == 0:
            src = noisy_ref.at[:, pl.ds(src_col, SIDE), :]
            dst = cols_out.at[1 if b < 0 else 0]
        else:
            src = noisy_ref.at[pl.ds(0 if a < 0 else rows - NEAR, NEAR), pl.ds(src_col, col_n), :]
            dst = rows_out.at[1 if a < 0 else 0, :, pl.ds(dst_col, col_n), :]
        copy = pltpu.make_async_remote_copy(
            src_ref=src, dst_ref=dst, send_sem=noisy_send.at[at], recv_sem=noisy_recv.at[at],
            device_id=beside(a, b), device_id_type=MESH,
        )
        copy.start()
        fields.append(copy)

    own.wait()
    for copy in gathers:
        copy.wait()
    conds = []
    for at, (a, b) in enumerate(DIRS):
        dst_lane = 2 * width if b < 0 else (0 if b > 0 else width)
        if a == 0:
            src_row, dst_row, row_n = DEEP, DEEP, rows
        else:
            src_row = DEEP if a < 0 else rows
            dst_row = DEEP + rows if a < 0 else 0
            row_n = DEEP
        copy = pltpu.make_async_remote_copy(
            src_ref=cond_out.at[pl.ds(src_row, row_n), :, pl.ds(width, width)],
            dst_ref=cond_out.at[pl.ds(dst_row, row_n), :, pl.ds(dst_lane, width)],
            send_sem=cond_send.at[at], recv_sem=cond_recv.at[at],
            device_id=beside(a, b), device_id_type=MESH,
        )
        copy.start()
        conds.append(copy)
    for copy in fields + conds:
        copy.wait()


def exchange(cond, noisy, members, strips, subs):
    share, _, width = cond.shape
    rows, cols, chans = noisy.shape
    dma = pltpu.SemaphoreType.DMA
    vmem = pl.BlockSpec(memory_space=pltpu.VMEM)
    return pl.pallas_call(
        functools.partial(exchange_kernel, members, strips, subs),
        out_shape=(
            jax.ShapeDtypeStruct((rows + 2 * DEEP, CH, 3 * width), jnp.bfloat16),
            jax.ShapeDtypeStruct((2, NEAR, cols + 2 * SIDE, chans), jnp.bfloat16),
            jax.ShapeDtypeStruct((2, rows, SIDE, chans), jnp.bfloat16),
        ),
        in_specs=[vmem, pl.BlockSpec(memory_space=pl.ANY)],
        out_specs=(vmem, vmem, vmem),
        scratch_shapes=[
            dma, dma((members,)), dma((members,)), dma((8,)), dma((8,)), dma((8,)), dma((8,)),
        ],
        compiler_params=pltpu.CompilerParams(collective_id=0, has_side_effects=True),
        name="exchange",
    )(cond, noisy)


def largest_part(count, most):
    return max(n for n in range(1, most + 1) if count % n == 0)


NT = (((1,), (1,)), ((), ()))
TN = (((0,), (1,)), ((), ()))


def network_kernel(
    bounds, scales, cond_ref, noisy_ref, rows_ref, cols_ref, w1_ref, w2_ref, wa_ref, wb_ref,
    b1_ref, b2_ref, ba_ref, out_ref, first, feats, field, hidden, k2, kn, kf, kb,
):
    rows, cols, chans = noisy_ref.shape
    span = cols + 2 * SIDE
    wide = 3 * chans

    def place(dst, src, start):
        dst[...] = jnp.zeros_like(dst)
        for out_row in range(2):
            for a in range(3):
                side, spot = divmod(out_row + a, 2)
                for b in range(3):
                    dst[side, out_row * chans:(out_row + 1) * chans,
                        spot * wide + b * chans:spot * wide + (b + 1) * chans] = (
                        src[3 * a + b, :, start:start + chans])

    place(k2, w2_ref, 0)
    place(kn, wa_ref, 0)
    place(kf, wa_ref, chans)
    place(kb, wb_ref, 0)

    col_at = lax.broadcasted_iota(jnp.int32, (span, chans), 0)
    inside_cols = (col_at >= bounds[2]) & (col_at < bounds[3])

    def masked(values, row):
        keep = inside_cols & (row >= bounds[0]) & (row < bounds[1])
        return jnp.where(keep, values, 0.0)

    def keep_shifted(dst, pair, spot, values):
        base = spot * wide
        dst[pair, :, base:base + chans] = pltpu.roll(values, 1, 0).astype(jnp.bfloat16)
        dst[pair, :, base + chans:base + 2 * chans] = values.astype(jnp.bfloat16)
        dst[pair, :, base + 2 * chans:base + wide] = pltpu.roll(values, span - 1, 0).astype(jnp.bfloat16)

    def silu(v):
        return v / (1.0 + jnp.exp(-v))

    def stage(pairs, most, product, finish):
        part = largest_part(pairs, most)

        def body(step, carry):
            start = step * part
            result = product(start, part)
            for p in range(part):
                for spot in range(2):
                    finish(start + p, spot,
                           result[p * span:(p + 1) * span, spot * chans:(spot + 1) * chans])
            return carry

        lax.fori_loop(0, pairs // part, body, 0)

    def conv(source, weight, start, part):
        low = source[pl.ds(start, part)].reshape(part * span, 2 * wide)
        high = source[pl.ds(start + 1, part)].reshape(part * span, 2 * wide)
        return (lax.dot_general(low, weight[0], NT, preferred_element_type=jnp.float32)
                + lax.dot_general(high, weight[1], NT, preferred_element_type=jnp.float32))

    half = rows // 2

    width3 = cond_ref.shape[2]
    b1 = b1_ref[...]
    lane_at = lax.broadcasted_iota(jnp.int32, (4 * CH, width3), 1) - (width3 // 3 - SIDE)
    inside_lanes = (lane_at >= bounds[2]) & (lane_at < bounds[3])
    line_at = lax.broadcasted_iota(jnp.int32, (4 * CH, width3), 0)

    def first_product(start, part):
        pieces = []
        for p in range(part):
            block = cond_ref[pl.ds(2 * (start + p), 4)].reshape(4 * CH, width3).astype(jnp.float32)
            top = 2 * (start + p) - DEEP
            keep = (inside_lanes & (line_at >= (bounds[0] - top) * CH)
                    & (line_at < (bounds[1] - top) * CH))
            block = jnp.where(keep, block, 0.0)
            shifted = [
                pltpu.roll(block, width3 - (cols - SIDE + b - 1), 1)[:, :span].astype(jnp.bfloat16)
                for b in range(3)
            ]
            left = jnp.concatenate(shifted, axis=0)
            pieces.append(lax.dot_general(left, w1_ref[...], TN, preferred_element_type=jnp.float32))
        return jnp.concatenate(pieces, axis=0) if part > 1 else pieces[0]

    def first_finish(pair, spot, values):
        keep_shifted(first, pair, spot, masked(silu(values + b1), 2 * pair + spot - 3))

    stage(half + 3, 1, first_product, first_finish)

    b2 = b2_ref[...]

    def feats_finish(pair, spot, values):
        keep_shifted(feats, pair, spot, masked(values + b2, 2 * pair + spot - 2))

    stage(half + 2, 2, lambda s, n: conv(first, k2, s, n), feats_finish)

    def scaled(values, row):
        return masked(scales[0] * values.astype(jnp.float32), row)

    for end in range(2):
        for r in range(NEAR):
            row = -NEAR + r if end == 0 else rows + r
            keep_shifted(field, (row + NEAR) // 2, (row + NEAR) % 2, scaled(rows_ref[end, r], row))

    def field_body(pair, carry):
        for spot in range(2):
            row = 2 * pair + spot
            values = jnp.concatenate(
                [cols_ref[0, row].astype(jnp.float32), noisy_ref[row].astype(jnp.float32),
                 cols_ref[1, row].astype(jnp.float32)], axis=0)
            keep_shifted(field, pair + 1, spot, scaled(values, row))
        return carry

    lax.fori_loop(0, half, field_body, 0)

    ba = ba_ref[...]

    def hidden_finish(pair, spot, values):
        keep_shifted(hidden, pair, spot, masked(silu(values + ba), 2 * pair + spot - 1))

    stage(half + 1, 3, lambda s, n: conv(field, kn, s, n) + conv(feats, kf, s, n), hidden_finish)

    def out_finish(pair, spot, values):
        row = 2 * pair + spot
        kept = scales[1] * noisy_ref[row].astype(jnp.float32)
        out_ref[row] = (kept + scales[2] * values[SIDE:SIDE + cols]).astype(jnp.bfloat16)

    stage(half, 2, lambda s, n: conv(hidden, kb, s, n), out_finish)


def network(bounds, scales, cond, noisy, row_ends, col_ends, w1, w2, wa, wb, b1, b2, ba):
    rows, cols, chans = noisy.shape
    span = cols + 2 * SIDE
    half = rows // 2
    vmem = pl.BlockSpec(memory_space=pltpu.VMEM)
    smem = pl.BlockSpec(memory_space=pltpu.SMEM)

    def held(pairs):
        return pltpu.VMEM((pairs, span, 6 * chans), jnp.bfloat16)

    return pl.pallas_call(
        network_kernel,
        out_shape=jax.ShapeDtypeStruct((rows, cols, chans), jnp.bfloat16),
        in_specs=[smem, smem] + [vmem] * 11,
        out_specs=vmem,
        scratch_shapes=[held(half + 3), held(half + 2), held(half + 2), held(half + 1)]
        + [pltpu.VMEM((2, 2 * chans, 6 * chans), jnp.bfloat16)] * 4,
        compiler_params=pltpu.CompilerParams(vmem_limit_bytes=60 * 1024 * 1024),
        name="network",
    )(bounds, scales, cond, noisy, row_ends, col_ends, w1, w2, wa, wb, b1, b2, ba)


def local(
    members, strips, subs,
    noisy, condition, levels, enc_w1, enc_b1, enc_w2, enc_b2, den_wa, den_ba, noise_gain, den_wb
):
    field = jnp.transpose(noisy[0], (1, 2, 0))
    rows, cols, chans = field.shape
    inputs = condition.shape[0]
    cond = jnp.pad(jnp.transpose(condition, (1, 0, 2)), ((0, 0), (0, CH - inputs), (0, 0)))
    cond_all, row_ends, col_ends = exchange(cond, field, members, strips, subs)

    level_value = levels[0].astype(jnp.float32)
    noise_sigma = SIG_LOW * (SIG_HIGH / SIG_LOW) ** (level_value / (LEVELS - 1))
    spread = noise_sigma * noise_sigma + SIGMA_DATA * SIGMA_DATA
    c_in = 1.0 / jnp.sqrt(spread)
    c_skip = SIGMA_DATA * SIGMA_DATA / spread
    c_out = noise_sigma * SIGMA_DATA / jnp.sqrt(spread)
    c_noise = jnp.log(noise_sigma) / 4.0
    scales = jnp.stack([c_in, c_skip, c_out])
    offset_a = (den_ba + c_noise * noise_gain)[None]

    strip = lax.axis_index("strip")
    sub = lax.axis_index("sub")
    bounds = jnp.stack([
        -strip * rows, (strips - strip) * rows,
        SIDE - sub * cols, SIDE + (subs - sub) * cols,
    ]).astype(jnp.int32)

    w1 = jnp.pad(enc_w1, ((0, 0), (0, 0), (0, CH - inputs))).reshape(3, 3, chans, CH)
    w1 = jnp.transpose(w1, (2, 1, 0, 3))
    w1 = jnp.concatenate([
        jnp.pad(w1, ((0, 0), (0, 0), (0, 1), (0, 0))),
        jnp.pad(w1, ((0, 0), (0, 0), (1, 0), (0, 0))),
    ], axis=0).reshape(2 * chans, 12 * CH)

    out = network(bounds, scales, cond_all, field, row_ends, col_ends, w1, enc_w2, den_wa, den_wb,
                  enc_b1[None], enc_b2[None], offset_a)
    return jnp.transpose(out, (2, 0, 1))[None]


def solution(mesh):
    return jax.shard_map(
        functools.partial(local, mesh.shape["member"], mesh.shape["strip"], mesh.shape["sub"]),
        mesh=mesh,
        in_specs=(
            P(("group", "member"), None, "strip", "sub"),
            P("group", ("strip", "member"), "sub"),
            P(("group", "member")),
            P(), P(), P(), P(), P(), P(), P(), P(),
        ),
        out_specs=P(("group", "member"), None, "strip", "sub"),
        check_vma=False,
    )
```

```python
import functools
import math

import jax
import jax.numpy as jnp
from jax import lax
from jax.experimental import pallas as pl
from jax.experimental.pallas import tpu as pltpu
from jax.sharding import PartitionSpec as P

LEVELS = 18
SIGMA_DATA = 0.5
SIG_LOW = 0.25
SIG_HIGH = 4.0
SIDE = 8
DEEP = 4
NEAR = 2
CH = 16
MESH = pl.DeviceIdType.MESH
DIRS = [(a, b) for a in (-1, 0, 1) for b in (-1, 0, 1) if (a, b) != (0, 0)]


def exchange_kernel(
    members, strips, subs, cond_ref, noisy_ref, cond_out, rows_out, cols_out,
    own_sem, gather_send, gather_recv, cond_send, cond_recv, noisy_send, noisy_recv,
):
    member = lax.axis_index("member")
    strip = lax.axis_index("strip")
    sub = lax.axis_index("sub")
    share, _, width = cond_ref.shape
    rows = share * members
    cols = noisy_ref.shape[1]

    def exists(a, b):
        held = (strip + a >= 0) & (strip + a < strips)
        return held & (sub + b >= 0) & (sub + b < subs)

    def beside(a, b):
        return {
            "strip": lax.rem(strip + a + strips, strips),
            "sub": lax.rem(sub + b + subs, subs),
        }

    mine = cond_out.at[pl.ds(DEEP + member * share, share), :, pl.ds(width, width)]
    own = pltpu.make_async_copy(cond_ref, mine, own_sem)
    own.start()

    barrier = pltpu.get_barrier_semaphore()
    for step in range(1, members):
        pl.semaphore_signal(
            barrier, inc=1, device_id={"member": lax.rem(member + step, members)},
            device_id_type=MESH,
        )
    for a, b in DIRS:
        pl.semaphore_signal(barrier, inc=1, device_id=beside(a, b), device_id_type=MESH)
    pl.semaphore_wait(barrier, members - 1 + len(DIRS))

    gathers = []
    for step in range(1, members):
        copy = pltpu.make_async_remote_copy(
            src_ref=cond_ref, dst_ref=mine,
            send_sem=gather_send.at[step], recv_sem=gather_recv.at[step],
            device_id={"member": lax.rem(member + step, members)}, device_id_type=MESH,
        )
        copy.start()
        gathers.append(copy)

    def start_if_there(copies, at, a, b, **refs):
        copy = pltpu.make_async_remote_copy(
            device_id=beside(a, b), device_id_type=MESH, **refs)

        @pl.when(exists(a, b))
        def _():
            copy.start()

        copies.append((copy, a, b))

    fields = []
    for at, (a, b) in enumerate(DIRS):
        src_col = cols - SIDE if b > 0 else 0
        dst_col = SIDE + cols if b < 0 else (0 if b > 0 else SIDE)
        col_n = SIDE if b else cols
        if a == 0:
            src = noisy_ref.at[:, pl.ds(src_col, SIDE), :]
            dst = cols_out.at[1 if b < 0 else 0]
        else:
            src = noisy_ref.at[pl.ds(0 if a < 0 else rows - NEAR, NEAR), pl.ds(src_col, col_n), :]
            dst = rows_out.at[1 if a < 0 else 0, :, pl.ds(dst_col, col_n), :]
        start_if_there(fields, at, a, b, src_ref=src, dst_ref=dst,
                       send_sem=noisy_send.at[at], recv_sem=noisy_recv.at[at])

    own.wait()
    for copy in gathers:
        copy.wait()
    conds = []
    for at, (a, b) in enumerate(DIRS):
        dst_lane = 2 * width if b < 0 else (0 if b > 0 else width)
        if a == 0:
            src_row, dst_row, row_n = DEEP, DEEP, rows
        else:
            src_row = DEEP if a < 0 else rows
            dst_row = DEEP + rows if a < 0 else 0
            row_n = DEEP
        start_if_there(
            conds, at, a, b,
            src_ref=cond_out.at[pl.ds(src_row, row_n), :, pl.ds(width, width)],
            dst_ref=cond_out.at[pl.ds(dst_row, row_n), :, pl.ds(dst_lane, width)],
            send_sem=cond_send.at[at], recv_sem=cond_recv.at[at])
    for copy, a, b in fields + conds:
        @pl.when(exists(a, b))
        def _(copy=copy):
            copy.wait_send()

        @pl.when(exists(-a, -b))
        def _(copy=copy):
            copy.wait_recv()


def exchange(cond, noisy, members, strips, subs):
    share, _, width = cond.shape
    rows, cols, chans = noisy.shape
    dma = pltpu.SemaphoreType.DMA
    vmem = pl.BlockSpec(memory_space=pltpu.VMEM)
    return pl.pallas_call(
        functools.partial(exchange_kernel, members, strips, subs),
        out_shape=(
            jax.ShapeDtypeStruct((rows + 2 * DEEP, CH, 3 * width), jnp.bfloat16),
            jax.ShapeDtypeStruct((2, NEAR, cols + 2 * SIDE, chans), jnp.bfloat16),
            jax.ShapeDtypeStruct((2, rows, SIDE, chans), jnp.bfloat16),
        ),
        in_specs=[vmem, pl.BlockSpec(memory_space=pl.ANY)],
        out_specs=(vmem, vmem, vmem),
        scratch_shapes=[
            dma, dma((members,)), dma((members,)), dma((8,)), dma((8,)), dma((8,)), dma((8,)),
        ],
        compiler_params=pltpu.CompilerParams(collective_id=0, has_side_effects=True),
        name="exchange",
    )(cond, noisy)


def largest_part(count, most):
    return max(n for n in range(1, most + 1) if count % n == 0)


NT = (((1,), (1,)), ((), ()))
TN = (((0,), (1,)), ((), ()))


def network_kernel(
    strips, subs, levels, cond_ref, noisy_ref, rows_ref, cols_ref, w1_ref, w2_ref, wa_ref, wb_ref,
    b1_ref, b2_ref, ba_ref, gain_ref, out_ref, lines, first, feats, field, hidden, k2, kn, kf, kb,
):
    rows, cols, chans = noisy_ref.shape
    span = cols + 2 * SIDE
    wide = 3 * chans
    half = rows // 2
    strip = lax.axis_index("strip")
    sub = lax.axis_index("sub")
    row_low, row_high = -strip * rows, (strips - strip) * rows
    col_low, col_high = SIDE - sub * cols, SIDE + (subs - sub) * cols

    level = jnp.full((1, chans), levels[0], jnp.int32).astype(jnp.float32)
    sigma = SIG_LOW * jnp.exp(level / (LEVELS - 1) * math.log(SIG_HIGH / SIG_LOW))
    spread = sigma * sigma + SIGMA_DATA * SIGMA_DATA
    c_in = 1.0 / jnp.sqrt(spread)
    c_skip = SIGMA_DATA * SIGMA_DATA / spread
    c_out = sigma * SIGMA_DATA / jnp.sqrt(spread)
    c_noise = jnp.log(sigma) / 4.0
    b1 = b1_ref[...]
    b2 = b2_ref[...]
    ba = ba_ref[...] + c_noise * gain_ref[...]

    def place(dst, src, start):
        for out_row in range(2):
            dst[1 - out_row, out_row * chans:(out_row + 1) * chans,
                (1 - out_row) * wide:(2 - out_row) * wide] = jnp.zeros((chans, wide), jnp.bfloat16)
            for a in range(3):
                side, spot = divmod(out_row + a, 2)
                for b in range(3):
                    dst[side, out_row * chans:(out_row + 1) * chans,
                        spot * wide + b * chans:spot * wide + (b + 1) * chans] = (
                        src[3 * a + b, :, start:start + chans])

    place(k2, w2_ref, 0)
    place(kn, wa_ref, 0)
    place(kf, wa_ref, chans)
    place(kb, wb_ref, 0)

    col_at = lax.broadcasted_iota(jnp.int32, (span, chans), 0)
    inside_cols = (col_at >= col_low) & (col_at < col_high)

    def masked(values, row):
        keep = (row >= row_low) & (row < row_high)
        left = jnp.where(inside_cols[:SIDE] & keep, values[:SIDE], 0.0)
        right = jnp.where(inside_cols[SIDE + cols:] & keep, values[SIDE + cols:], 0.0)
        middle = jnp.where(keep, values[SIDE:SIDE + cols], 0.0)
        return jnp.concatenate([left, middle, right], axis=0)

    def keep_shifted(dst, pair, spot, values):
        base = spot * wide
        dst[pair, :, base:base + chans] = pltpu.roll(values, 1, 0).astype(jnp.bfloat16)
        dst[pair, :, base + chans:base + 2 * chans] = values.astype(jnp.bfloat16)
        dst[pair, :, base + 2 * chans:base + wide] = pltpu.roll(values, span - 1, 0).astype(jnp.bfloat16)

    def silu(v):
        h = 0.5 * v
        return h * jnp.tanh(h) + h

    def conv(source, weight, pair, part, low, high):
        left = source[pl.ds(pair, part), low:high].reshape(part * (high - low), 2 * wide)
        right = source[pl.ds(pair + 1, part), low:high].reshape(part * (high - low), 2 * wide)
        return (lax.dot_general(left, weight[0], NT, preferred_element_type=jnp.float32)
                + lax.dot_general(right, weight[1], NT, preferred_element_type=jnp.float32))

    def rows_of(result, part):
        height = result.shape[0] // part
        for p in range(part):
            for spot in range(2):
                yield p, spot, result[p * height:(p + 1) * height, spot * chans:(spot + 1) * chans]

    def run(count, most, *stages):
        part = largest_part(count, most)

        def body(step, carry):
            for stage in stages:
                stage(step * part, part)
            return carry

        lax.fori_loop(0, count // part, body, 0)

    width3 = cond_ref.shape[2]
    lane_at = lax.broadcasted_iota(jnp.int32, (2 * CH, width3), 1) - (width3 // 3 - SIDE)
    inside_lanes = (lane_at >= col_low) & (lane_at < col_high)

    def lines_stage(pair):
        row = 2 * pair - DEEP
        keep = inside_lanes & (row >= row_low) & (row < row_high)
        block = cond_ref[pl.ds(2 * pair, 2)].reshape(2 * CH, width3).astype(jnp.float32)
        block = jnp.where(keep, block, 0.0)
        for b in range(3):
            moved = pltpu.roll(block, width3 - (cols - SIDE + b - 1), 1)[:, :2 * chans]
            lines[pair, 2 * CH * b:2 * CH * (b + 1)] = moved.astype(jnp.bfloat16)

    def first_stage(pair):
        left = jnp.concatenate([lines[pair], lines[pair + 1]], axis=0)[:, :span]
        result = lax.dot_general(left, w1_ref[...], TN, preferred_element_type=jnp.float32)
        for spot in range(2):
            values = silu(result[:, spot * chans:(spot + 1) * chans] + b1)
            keep_shifted(first, pair, spot, masked(values, 2 * pair + spot - 3))

    def feats_stage(pair, part):
        result = conv(first, k2, pair, part, 0, span)
        for p, spot, values in rows_of(result, part):
            row = 2 * (pair + p) + spot - 2
            keep_shifted(feats, pair + p, spot, masked(values + b2, row))

    def scaled(values, row):
        return masked(c_in * values.astype(jnp.float32), row)

    for end in range(2):
        for r in range(NEAR):
            row = -NEAR + r if end == 0 else rows + r
            keep_shifted(field, (row + NEAR) // 2, (row + NEAR) % 2, scaled(rows_ref[end, r], row))

    def field_stage(pair):
        for spot in range(2):
            row = 2 * pair + spot - NEAR
            values = jnp.concatenate(
                [cols_ref[0, row].astype(jnp.float32), noisy_ref[row].astype(jnp.float32),
                 cols_ref[1, row].astype(jnp.float32)], axis=0)
            keep_shifted(field, pair, spot, scaled(values, row))

    def hidden_stage(pair, part):
        result = conv(field, kn, pair, part, 0, span) + conv(feats, kf, pair, part, 0, span)
        for p, spot, values in rows_of(result, part):
            row = 2 * (pair + p) + spot - 1
            keep_shifted(hidden, pair + p, spot, masked(silu(values + ba), row))

    def out_stage(pair, part):
        result = conv(hidden, kb, pair, part, SIDE, SIDE + cols)
        for p, spot, values in rows_of(result, part):
            row = 2 * (pair + p) + spot
            kept = c_skip * noisy_ref[row].astype(jnp.float32)
            out_ref[row] = (kept + c_out * values).astype(jnp.bfloat16)

    def each(stage):
        def several(pair, part):
            for p in range(part):
                stage(pair + p)
        return several

    run(half + DEEP, 4, each(lines_stage))
    run(half + 3, 5, each(first_stage))
    run(half + 2, 2, feats_stage)
    run(half, 4, lambda pair, part: each(field_stage)(pair + 1, part))
    run(half + 1, 3, hidden_stage)
    run(half, 4, out_stage)


def network(strips, subs, levels, cond, noisy, row_ends, col_ends, w1, w2, wa, wb, b1, b2, ba, gain):
    rows, cols, chans = noisy.shape
    span = cols + 2 * SIDE
    half = rows // 2
    vmem = pl.BlockSpec(memory_space=pltpu.VMEM)
    smem = pl.BlockSpec(memory_space=pltpu.SMEM)

    def held(pairs):
        return pltpu.VMEM((pairs, span, 6 * chans), jnp.bfloat16)

    return pl.pallas_call(
        functools.partial(network_kernel, strips, subs),
        out_shape=jax.ShapeDtypeStruct((rows, cols, chans), jnp.bfloat16),
        in_specs=[smem] + [vmem] * 12,
        out_specs=vmem,
        scratch_shapes=[pltpu.VMEM((half + DEEP, 6 * CH, 2 * chans), jnp.bfloat16)]
        + [held(half + 3), held(half + 2), held(half + 2), held(half + 1)]
        + [pltpu.VMEM((2, 2 * chans, 6 * chans), jnp.bfloat16)] * 4,
        compiler_params=pltpu.CompilerParams(vmem_limit_bytes=60 * 1024 * 1024),
        name="network",
    )(levels, cond, noisy, row_ends, col_ends, w1, w2, wa, wb, b1, b2, ba, gain)


def local(
    members, strips, subs,
    noisy, condition, levels, enc_w1, enc_b1, enc_w2, enc_b2, den_wa, den_ba, noise_gain, den_wb
):
    field = jnp.transpose(noisy[0], (1, 2, 0))
    rows, cols, chans = field.shape
    inputs = condition.shape[0]
    cond = jnp.pad(jnp.transpose(condition, (1, 0, 2)), ((0, 0), (0, CH - inputs), (0, 0)))
    cond_all, row_ends, col_ends = exchange(cond, field, members, strips, subs)

    w1 = jnp.pad(enc_w1, ((0, 0), (0, 0), (0, CH - inputs))).reshape(3, 3, chans, CH)
    w1 = jnp.transpose(w1, (2, 1, 0, 3))
    w1 = jnp.concatenate([
        jnp.pad(w1, ((0, 0), (0, 0), (0, 1), (0, 0))),
        jnp.pad(w1, ((0, 0), (0, 0), (1, 0), (0, 0))),
    ], axis=0).reshape(2 * chans, 3, 2, 2 * CH)
    w1 = jnp.transpose(w1, (0, 2, 1, 3)).reshape(2 * chans, 12 * CH)

    out = network(strips, subs, levels, cond_all, field, row_ends, col_ends, w1, enc_w2, den_wa, den_wb,
                  enc_b1[None], enc_b2[None], den_ba[None], noise_gain[None])
    return jnp.transpose(out, (2, 0, 1))[None]


def solution(mesh):
    return jax.shard_map(
        functools.partial(local, mesh.shape["member"], mesh.shape["strip"], mesh.shape["sub"]),
        mesh=mesh,
        in_specs=(
            P(("group", "member"), None, "strip", "sub"),
            P("group", ("strip", "member"), "sub"),
            P(("group", "member")),
            P(), P(), P(), P(), P(), P(), P(), P(),
        ),
        out_specs=P(("group", "member"), None, "strip", "sub"),
        check_vma=False,
    )
```
